32 devices in a mesh: fsdp: 8 (over z, x), tp: 4 (over y, core).
Axes of the slice: x: 2, y: 2, z: 4, core: 2. Of those that a mesh axis runs over, the one named last changes fastest.
Arguments:
- inputs: bfloat16 [8192, 2048], P(('fsdp', 'tp')), may hold values from -6 to 6
- teacher: bfloat16 [8192, 2048], P(('fsdp', 'tp')), may hold values from -6 to 6
- gain_attn: bfloat16 [2048], P('fsdp'), may hold values from 0.099609375 to 1.8984375
- gain_mlp: bfloat16 [2048], P('fsdp'), may hold values from 0.099609375 to 1.8984375
- w_query: bfloat16 [2048, 2048], P('fsdp', 'tp'), may hold values from -0.125 to 0.125
- w_key: bfloat16 [2048, 512], P('fsdp', 'tp'), may hold values from -0.125 to 0.125
- w_value: bfloat16 [2048, 512], P('fsdp', 'tp'), may hold values from -0.125 to 0.125
- w_out: bfloat16 [2048, 2048], P('tp', 'fsdp'), may hold values from -2 to 2
- w_gate: bfloat16 [2048, 8192], P('fsdp', 'tp'), may hold values from -0.125 to 0.125
- w_up: bfloat16 [2048, 8192], P('fsdp', 'tp'), may hold values from -0.125 to 0.125
- w_down: bfloat16 [8192, 2048], P('tp', 'fsdp'), may hold values from -0.0625 to 0.0625
- position: int32 [8, 1024], P('fsdp'), may hold values from 0 to 1023, each once within a row
- documents: int32 [8, 1024], P('fsdp'), may hold values from 0 to 3, never falling along the last dimension, each value on 1 to 512 neighbouring positions
- lengths: int32 [8], P('fsdp'), may hold values from 1 to 1024, as said below
Outputs:
- outputs: bfloat16 [8192, 2048], P(('fsdp', 'tp'))
- grad_inputs: float32 [8192, 2048], P(('fsdp', 'tp'))
- grad_gain_attn: float32 [2048], P(('fsdp', 'tp'))
- grad_gain_mlp: float32 [2048], P(('fsdp', 'tp'))
- grad_w_query: float32 [2048, 2048], P('fsdp', 'tp')
- grad_w_key: float32 [2048, 512], P('fsdp', 'tp')
- grad_w_value: float32 [2048, 512], P('fsdp', 'tp')
- grad_w_out: float32 [2048, 2048], P('tp', 'fsdp')
- grad_w_gate: float32 [2048, 8192], P('fsdp', 'tp')
- grad_w_up: float32 [2048, 8192], P('fsdp', 'tp')
- grad_w_down: float32 [8192, 2048], P('tp', 'fsdp')
The draws below stay inside these ranges and needn't reach their ends.
Inputs may be any that keep to these rules, and one draw needn't show every extreme that they name: Each row of position holds every place 0 to 1023 once. `documents`: non-decreasing along the places of a sequence; each of the 4 documents of a sequence holds 1 to 512 places, one exactly 512. `lengths`: one sequence of every draw is full.
All inputs are finite; a program needn't handle non-finite values.
Results may differ from the reference program's by a relative error of at most 0.014.
Values may be sent and summed in bfloat16 or wider, within the bound.
No kernel may reach another device: no remote copies, remote signals or barrier semaphores. Data moves between devices by JAX's collectives and lax.ppermute only.
A program may use at most 256 MiB of HBM per device.

```python
import math
import jax
import jax.numpy as jnp
import numpy as np
from jax import lax

D = 2048
H = 32
KV = 8
HD = 64
FF = 8192
DOCS = 4
PACK = 1024
SEQS = 8
TOKENS = 8192


def draw_lengths(key, part):
    seq_index = jnp.arange(SEQS, dtype=jnp.int32)
    rising = 3 * PACK // 10 + 7 * PACK * seq_index // (10 * max(SEQS - 1, 1))
    jitter = jax.random.randint(jax.random.fold_in(key, 1), (SEQS,), 0, max(PACK // 16, 1) + 1)
    full_seq = jax.random.randint(jax.random.fold_in(key, 2), (), 0, SEQS)
    clipped = jnp.clip(rising - jitter, 1, PACK)
    return jnp.where(seq_index == full_seq, PACK, clipped).astype(jnp.int32)


def steps_of(rng, dims, split, smallest, high):
    level = 1.0
    for dim, parts in split:
        heights = jax.random.uniform(jax.random.fold_in(jax.random.fold_in(rng, 6), dim), (parts,), jnp.float32, smallest / len(split), high / len(split))
        level = level * jnp.repeat(jnp.exp(heights), dims[dim] // parts).reshape((-1,) + (1,) * (len(dims) - 1 - dim))
    return level


def split_up(number_of, total, limit, skew):
    loads = [(1 << 20) // math.isqrt(standing ** skew) + 1 for standing in range(2, number_of + 1)]
    surplus, counts = total - limit - (number_of - 1), [1] * (number_of - 1)
    while surplus > 0:
        free = [i for i in range(number_of - 1) if counts[i] < limit]
        pool, budget = sum([loads[i] for i in free]), surplus
        for i in free:
            more = min(limit - counts[i], max(1, budget * loads[i] // pool), surplus)
            counts[i] = counts[i] + more
            surplus = surplus - more
    return np.array([limit] + counts)


def uneven_parts(own_key, number_of, total, reach, slope):
    if number_of == 2:
        one = jax.random.randint(own_key, (), max(1, total - reach), min(reach, total - 1) + 1)
        return jnp.stack([one, total - one])
    tallies = jnp.asarray(split_up(number_of, total, reach, slope), jnp.int32)
    pairs = (number_of - 1) // 2
    source_of, taker = tallies[1:1 + 2 * pairs:2], tallies[2:2 + 2 * pairs:2]
    room = jnp.minimum(source_of - 1, reach - taker)
    passed = jax.random.randint(jax.random.fold_in(own_key, 1), (pairs,), 0, 1 << 20) % (room + 1)
    tallies = tallies.at[1:1 + 2 * pairs:2].set(source_of - passed).at[2:2 + 2 * pairs:2].set(taker + passed)
    return tallies[jax.random.permutation(jax.random.fold_in(own_key, 2), number_of)]


def noise(key, shape, width, reach, shards=(), kind=jnp.bfloat16):
    drawn = jax.random.normal(key, shape, jnp.float32) * width
    if len(shards) > 0:
        drawn = steps_of(key, shape, shards, -0.22, 0.18) * drawn
    return jnp.clip(drawn, min=-reach, max=reach).astype(kind)


def setup_inputs(seed: int = 0) -> dict:
    streams_of = jax.random.split(jax.random.key(seed), 15)
    inputs = noise(streams_of[0], (TOKENS, D), 1.0, 6.0, ((0, 32),))
    teacher = noise(streams_of[1], (TOKENS, D), 1.0, 6.0, ((0, 32),))
    gain_attn = jnp.clip(1.0 + 0.18 * jax.random.normal(streams_of[2], (D,), jnp.float32), 0.099609375, 1.8984375).astype(jnp.bfloat16)
    gain_mlp = jnp.clip(1.0 + 0.18 * jax.random.normal(streams_of[3], (D,), jnp.float32), 0.099609375, 1.8984375).astype(jnp.bfloat16)
    w_query = noise(streams_of[4], (D, H * HD), D ** -0.5, 0.125, ((0, 8), (1, 4)))
    w_key = noise(streams_of[5], (D, KV * HD), D ** -0.5, 0.125, ((0, 8), (1, 4)))
    w_value = noise(streams_of[6], (D, KV * HD), D ** -0.5, 0.125, ((0, 8), (1, 4)))
    w_out = noise(streams_of[7], (H * HD, D), (max(H * HD * DOCS // PACK, 4)) ** -0.5, 2.0, ((0, 4), (1, 8)))
    w_gate = noise(streams_of[8], (D, FF), D ** -0.5, 0.125, ((0, 8), (1, 4)))
    w_up = noise(streams_of[9], (D, FF), D ** -0.5, 0.125, ((0, 8), (1, 4)))
    w_down = noise(streams_of[10], (FF, D), FF ** -0.5, 0.0625, ((0, 4), (1, 8)))
    position = jax.vmap(lambda own: jax.random.permutation(own, PACK))(jax.random.split(streams_of[11], SEQS)).reshape((SEQS, PACK)).astype(jnp.int32)
    documents = jax.vmap(lambda own: jnp.searchsorted(jnp.cumsum(uneven_parts(own, DOCS, PACK, PACK // 2, 2)), jnp.arange(PACK), side="right"))(jax.random.split(streams_of[12], SEQS)).reshape((SEQS, PACK)).astype(jnp.int32)
    lengths = draw_lengths(jax.random.fold_in(streams_of[14], 71), 0)
    return dict(inputs=inputs, teacher=teacher, gain_attn=gain_attn, gain_mlp=gain_mlp, w_query=w_query, w_key=w_key, w_value=w_value, w_out=w_out, w_gate=w_gate, w_up=w_up, w_down=w_down, position=position, documents=documents, lengths=lengths)


HIGHEST = lax.Precision.HIGHEST
epsilon = 1e-05

@jax.custom_vjp
def low(v):
    return lax.optimization_barrier(v.astype(jnp.bfloat16)).astype(jnp.float32)

@jax.custom_vjp
def low_back(v):
    return v

def low_keep(v):
    return (low(v), None)

def low_pass(kept, grad):
    return (grad,)

def back_keep(v):
    return (v, None)

def back_low(kept, grad):
    return (low(grad),)
low.defvjp(low_keep, low_pass)
low_back.defvjp(back_keep, back_low)

def rope_freqs(head_size):
    base = 1.0 / 500000.0 ** (np.arange(0, head_size, 2) / head_size)
    wavelen = 2.0 * math.pi / base
    smooth = (8192.0 / wavelen - 1.0) / 3.0
    mixed = (1.0 - smooth) * base / 32.0 + smooth * base
    scaled = np.where(wavelen > 8192.0, base / 32.0, np.where(wavelen < 2048.0, base, mixed))
    return jnp.asarray(scaled, dtype=jnp.float32)

def rope_tables(place, head_size):
    angle = place.astype(jnp.float32)[:, None] * rope_freqs(head_size)[None, :]
    cosine = jnp.concatenate([jnp.cos(angle), jnp.cos(angle)], axis=-1)
    sine = jnp.concatenate([jnp.sin(angle), jnp.sin(angle)], axis=-1)
    return (cosine, sine)

def rotate(values, cosine, sine):
    half = values.shape[-1] // 2
    turned = jnp.concatenate([-values[..., half:], values[..., :half]], axis=-1)
    return values * cosine[:, None, :] + turned * sine[:, None, :]

def rms_norm(values, gain):
    return values * lax.rsqrt(lax.optimization_barrier(jnp.mean(values * values, axis=-1, keepdims=True)) + epsilon) * gain

def exact_dot(left, right):
    return jnp.dot(left, right, precision=HIGHEST)

def attend(query, keys, values, place, label):
    group_size = H // KV
    block_rows = min(512, PACK)
    blocks = PACK // block_rows
    query_blocks = query.reshape(blocks, block_rows, KV, group_size, HD)
    place_blocks = place.reshape(blocks, block_rows)
    label_blocks = label.reshape(blocks, block_rows)

    def one_block(item):
        query_part, place_part, label_part = item
        scores = low_back(0.125 * jnp.einsum('bngd,snd->ngbs', query_part, keys, precision=HIGHEST))
        allowed = (label_part[:, None] == label[None, :]) & (place[None, :] <= place_part[:, None])
        scores = jnp.where(allowed[None, None], scores, -1e+30)
        row_max = lax.optimization_barrier(jnp.max(scores, axis=-1, keepdims=True))
        weights = jnp.exp(scores - row_max)
        probs = weights / lax.optimization_barrier(jnp.sum(weights, axis=-1, keepdims=True))
        return jnp.einsum('ngbs,snd->bngd', low(probs), values, precision=HIGHEST)
    result = lax.map(jax.checkpoint(one_block), (query_blocks, place_blocks, label_blocks))
    return result.reshape(PACK, H * HD)

def layer_pass(params, seq_inputs, seq_teacher, place, seq_docs, seq_length, scale):
    gain_attn, gain_mlp, w_query, w_key, w_value, w_out, w_gate, w_up, w_down = params
    label = jnp.take(seq_docs, place)
    valid = (place < seq_length).astype(jnp.float32)
    cosine, sine = rope_tables(place, HD)
    normed = low(rms_norm(seq_inputs, gain_attn))
    query = low(rotate(low_back(exact_dot(normed, w_query)).reshape(PACK, H, HD), cosine, sine))
    keys = low(rotate(low_back(exact_dot(normed, w_key)).reshape(PACK, KV, HD), cosine, sine))
    values = low(low_back(exact_dot(normed, w_value))).reshape(PACK, KV, HD)
    heads = low(low_back(attend(query, keys, values, place, label)))
    middle = seq_inputs + low_back(exact_dot(heads, w_out))
    normed_two = low(rms_norm(middle, gain_mlp))
    gate = low_back(exact_dot(normed_two, w_gate))
    upper = low_back(exact_dot(normed_two, w_up))
    hidden = low(jax.nn.silu(gate) * upper)
    result = middle + low_back(exact_dot(hidden, w_down))
    loss_part = scale * jnp.sum(valid[:, None] * (result - seq_teacher) ** 2)
    return (loss_part, result)

def forward(params, inputs32, teacher32, position, documents, lengths, scale):
    layer_saved = jax.checkpoint(layer_pass)
    input_seqs = inputs32.reshape(SEQS, PACK, D)
    teacher_seqs = teacher32.reshape(SEQS, PACK, D)

    def seq_step(loss_sum, item):
        loss_part, result = layer_saved(params, item[0], item[1], item[2], item[3], item[4], scale)
        return (loss_sum + loss_part, result)
    loss_sum, results = lax.scan(seq_step, jnp.zeros((), jnp.float32), (input_seqs, teacher_seqs, position, documents, lengths))
    return (loss_sum, results.reshape(TOKENS, D))

def to_given(rows, position):
    inverse = jnp.argsort(position, axis=1).astype(jnp.int32)
    seq_rows = rows.reshape(SEQS, PACK, D)
    return jnp.take_along_axis(seq_rows, inverse[:, :, None], axis=1).reshape(TOKENS, D)

def reference(inputs, teacher, gain_attn, gain_mlp, w_query, w_key, w_value, w_out, w_gate, w_up, w_down, position, documents, lengths):
    valid = (position < lengths[:, None]).astype(jnp.float32)
    count = jnp.sum(valid)
    scale = TOKENS / (2.0 * count)
    params = tuple((item.astype(jnp.float32) for item in (gain_attn, gain_mlp, w_query, w_key, w_value, w_out, w_gate, w_up, w_down)))
    inputs32 = inputs.astype(jnp.float32)
    teacher32 = teacher.astype(jnp.float32)

    def loss_of(params_in, inputs_in):
        return forward(params_in, inputs_in, teacher32, position, documents, lengths, scale)
    (loss_sum, result), pull = jax.vjp(loss_of, params, inputs32)
    grads, grad_inputs = pull((jnp.ones((), jnp.float32), jnp.zeros_like(result)))
    return (to_given(result, position).astype(jnp.bfloat16), to_given(grad_inputs, position), grads[0], grads[1], grads[2], grads[3], grads[4], grads[5], grads[6], grads[7], grads[8])
```

```python
import math

import jax
import jax.numpy as jnp
import numpy as np
from jax import lax
from jax.sharding import PartitionSpec as P

HD = 64

epsilon = 1e-05
f32 = jnp.float32
bf16 = jnp.bfloat16


def rope_freqs(head_size):
    base = 1.0 / 500000.0 ** (np.arange(0, head_size, 2) / head_size)
    wavelen = 2.0 * math.pi / base
    smooth = (8192.0 / wavelen - 1.0) / 3.0
    mixed = (1.0 - smooth) * base / 32.0 + smooth * base
    scaled = np.where(wavelen > 8192.0, base / 32.0, np.where(wavelen < 2048.0, base, mixed))
    return jnp.asarray(scaled, dtype=jnp.float32)


def rope_tables(place, head_size):
    angle = place.astype(jnp.float32)[:, None] * rope_freqs(head_size)[None, :]
    cosine = jnp.concatenate([jnp.cos(angle), jnp.cos(angle)], axis=-1)
    sine = jnp.concatenate([jnp.sin(angle), jnp.sin(angle)], axis=-1)
    return (cosine, sine)


def rotate(values, cosine, sine):
    half = values.shape[-1] // 2
    turned = jnp.concatenate([-values[..., half:], values[..., :half]], axis=-1)
    return values * cosine[:, None, :] + turned * sine[:, None, :]


def rotate_back(grads, cosine, sine):
    half = grads.shape[-1] // 2
    turned = grads * sine[:, None, :]
    return grads * cosine[:, None, :] + jnp.concatenate(
        [turned[..., half:], -turned[..., :half]], axis=-1
    )


def rms_norm(values, gain):
    return values * lax.rsqrt(jnp.mean(values * values, axis=-1, keepdims=True) + epsilon) * gain


def norm_back(values, gain, upstream):
    factor = lax.rsqrt(jnp.mean(values * values, axis=-1, keepdims=True) + epsilon)
    normed = values * factor
    scaled = upstream * gain
    grad_values = factor * (scaled - normed * jnp.mean(scaled * normed, axis=-1, keepdims=True))
    return (grad_values, jnp.sum(upstream * normed, axis=0))


def matmul(left, right):
    return jnp.dot(left, right, preferred_element_type=jnp.float32)


def matmul_tn(left, right):
    return lax.dot_general(
        left, right, (((0,), (0,)), ((), ())), preferred_element_type=jnp.float32
    )


def matmul_nt(left, right):
    return lax.dot_general(
        left, right, (((1,), (1,)), ((), ())), preferred_element_type=jnp.float32
    )


class Ring:
    def __init__(self, axis):
        self.axis = axis
        self.ways = lax.axis_size(axis)
        ways = self.ways
        self.order = list(range(0, ways, 2)) + list(range(1, ways, 2))[::-1]
        self.place_of = [self.order.index(shard) for shard in range(ways)]
        self.place = jnp.asarray(self.place_of, jnp.int32)[lax.axis_index(axis)]
        self.up = [(self.order[i], self.order[(i + 1) % ways]) for i in range(ways)]
        self.down = [(b, a) for a, b in self.up]

    def to_ring(self, values):
        half = values.shape[1] // self.ways // 2
        order = jnp.asarray(self.order, jnp.int32)
        parts = []
        for side, sign in ((0, -1), (1, 1)):
            for step in range(self.ways):
                shard = order[(self.place + sign * step + self.ways) % self.ways]
                parts.append(
                    lax.dynamic_slice_in_dim(values, (shard * 2 + side) * half, half, axis=1)
                )
        return jnp.concatenate(parts, axis=1)

    def from_ring(self, values):
        half = values.shape[1] // self.ways // 2
        parts = []
        for shard in range(self.ways):
            ahead = (self.place - self.place_of[shard] + self.ways) % self.ways
            behind = (self.place_of[shard] - self.place + self.ways) % self.ways
            parts.append(lax.dynamic_slice_in_dim(values, ahead * half, half, axis=1))
            parts.append(lax.dynamic_slice_in_dim(values, (self.ways + behind) * half, half, axis=1))
        return jnp.concatenate(parts, axis=1)

    def gather(self, shard):
        half = shard.shape[0] // 2
        rising, falling = [shard[:half]], [shard[half:]]
        for _ in range(self.ways - 1):
            rising.append(lax.ppermute(rising[-1], self.axis, self.up))
            falling.append(lax.ppermute(falling[-1], self.axis, self.down))
        return jnp.concatenate(rising + falling, axis=0)

    def reduce(self, left, right):
        half = left.shape[1] // self.ways // 2
        sides = []
        for side, hop in ((0, self.up), (1, self.down)):
            total = None
            for step in range(self.ways):
                block = side * self.ways + (1 + step) % self.ways
                term = matmul_tn(left[:, block * half : (block + 1) * half], right)
                if total is not None:
                    term = term + lax.ppermute(total, self.axis, hop).astype(f32)
                total = term.astype(bf16) if step < self.ways - 1 else term
            sides.append(total)
        return jnp.concatenate(sides, axis=0)


def swap(values, axis, bit):
    return lax.ppermute(values, axis, [(i, i ^ bit) for i in range(lax.axis_size(axis))])


def butterfly(values, axis):
    bit = 1
    while bit < lax.axis_size(axis):
        values = values + swap(values, axis, bit)
        bit *= 2
    return values


def rows_gather(rows):
    across = swap(rows, "tp", 2)
    beside = swap(rows, "tp", 1)
    return jnp.concatenate([rows, beside, across, swap(across, "tp", 1)], axis=0)


def rows_reduce(far, near):
    rows = far.shape[0] // 2
    across = far[:rows] + swap(far[rows:].astype(bf16), "tp", 1).astype(f32)
    across = swap(across.astype(bf16), "tp", 2).astype(f32)
    return near[:rows] + swap(near[rows:].astype(bf16), "tp", 1).astype(f32) + across


def per_device(
    inputs,
    teacher,
    gain_attn,
    gain_mlp,
    w_query,
    w_key,
    w_value,
    w_out,
    w_gate,
    w_up,
    w_down,
    position,
    documents,
    lengths,
):
    row_count = inputs.shape[0]
    tp_ways = lax.axis_size("tp")
    pack_rows = row_count * tp_ways
    total_rows = pack_rows * lax.axis_size("fsdp")
    tp_index = lax.axis_index("tp")
    ring = Ring("fsdp")
    place = position[0]
    label = documents[0]

    def own_rows(values):
        return lax.dynamic_slice_in_dim(values, tp_index * row_count, row_count)

    def block_of(values, block):
        return lax.dynamic_slice_in_dim(
            values, (tp_index ^ block) * row_count, row_count
        )

    count = butterfly(jnp.clip(lengths, 0, pack_rows).astype(f32), "fsdp")[0]
    given = jnp.arange(pack_rows, dtype=jnp.int32)
    valid = (own_rows(given) < lengths[0]).astype(f32)
    cosine, sine = rope_tables(given, HD)

    q_cols, kv_cols, out_cols = w_query.shape[1], w_key.shape[1], w_out.shape[0]
    gains = jnp.stack([gain_attn, gain_mlp], axis=1)
    gains = jnp.pad(gains, ((0, 0), (0, 126)))
    attn_all = ring.gather(
        jnp.concatenate([w_query, w_key, w_value, w_out.T, gains], axis=1)
    )
    qkv_cols = q_cols + 2 * kv_cols
    qkv_all = attn_all[:, :qkv_cols]
    out_all = attn_all[:, qkv_cols : qkv_cols + out_cols]
    gain_one = attn_all[:, qkv_cols + out_cols].astype(f32)
    gain_two = attn_all[:, qkv_cols + out_cols + 1].astype(f32)
    gate_all = ring.gather(w_gate)
    up_all = ring.gather(w_up)
    down_all = ring.gather(w_down.T)

    place_blocks = jnp.concatenate([block_of(place, k) for k in range(tp_ways)])
    pick = (given[:, None] == place_blocks[None, :]).astype(bf16)
    held = rows_gather(ring.to_ring(inputs))
    inputs_full = matmul(pick, held)
    inputs32 = own_rows(inputs_full)
    normed_full = rms_norm(inputs_full, gain_one).astype(bf16)
    teacher_own = matmul(own_rows(pick), rows_gather(ring.to_ring(teacher)))

    heads_local = q_cols // HD
    kv_local = kv_cols // HD
    group_size = heads_local // kv_local
    qkv = matmul(normed_full, qkv_all)
    query = rotate(qkv[:, :q_cols].reshape(pack_rows, heads_local, HD), cosine, sine).astype(bf16)
    keys = rotate(
        qkv[:, q_cols : q_cols + kv_cols].reshape(pack_rows, kv_local, HD), cosine, sine
    ).astype(bf16)
    values = qkv[:, q_cols + kv_cols :].astype(bf16).reshape(pack_rows, kv_local, HD)
    block_rows = min(256, pack_rows)
    starts = list(range(0, pack_rows, block_rows))
    reach = pack_rows // 2

    def block_scores(first_row):
        first_key = max(0, first_row - reach)
        span = slice(first_key, first_row + block_rows)
        rows = slice(first_row, first_row + block_rows)
        query_part = query[rows].reshape(block_rows, kv_local, group_size, HD)
        scores = 0.125 * jnp.einsum(
            "bngd,snd->ngbs", query_part, keys[span], preferred_element_type=jnp.float32
        )
        allowed = (label[rows][:, None] == label[span][None, :]) & (
            given[span][None, :] <= given[rows][:, None]
        )
        return (query_part, span, jnp.where(allowed[None, None], scores, -1e30))

    head_parts = []
    log_sums = []
    for first_row in starts:
        query_part, span, scores = block_scores(first_row)
        row_max = jnp.max(scores, axis=-1, keepdims=True)
        weights = jnp.exp(scores - row_max)
        row_total = jnp.sum(weights, axis=-1, keepdims=True)
        probs = (weights / row_total).astype(jnp.bfloat16)
        mixed = jnp.einsum("ngbs,snd->bngd", probs, values[span], preferred_element_type=jnp.float32)
        head_parts.append(mixed.astype(jnp.bfloat16).reshape(block_rows, heads_local * HD))
        log_sums.append(row_max + jnp.log(row_total))
    heads = jnp.concatenate(head_parts, axis=0)

    heads_far = jnp.concatenate([block_of(heads, 2), block_of(heads, 3)], axis=0)
    heads_near = jnp.concatenate([block_of(heads, 0), block_of(heads, 1)], axis=0)
    middle = inputs32 + rows_reduce(matmul_nt(heads_far, out_all), matmul_nt(heads_near, out_all))
    normed_two = rms_norm(middle, gain_two).astype(bf16)
    normed_two_full = rows_gather(normed_two)
    gate = matmul(normed_two_full, gate_all)
    upper = matmul(normed_two_full, up_all)
    hidden = (jax.nn.silu(gate) * upper).astype(bf16)
    near_rows = 2 * row_count
    result = middle + rows_reduce(
        matmul_nt(hidden[near_rows:], down_all), matmul_nt(hidden[:near_rows], down_all)
    )
    grad_out = total_rows / count * valid[:, None] * (result - teacher_own)
    grad_out_full = rows_gather(grad_out.astype(bf16))
    grad_down = ring.reduce(grad_out_full, hidden)
    grad_hidden = matmul(grad_out_full, down_all)
    sigma = jax.nn.sigmoid(gate)
    grad_gate = (grad_hidden * upper * sigma * (1.0 + gate * (1.0 - sigma))).astype(bf16)
    grad_upper = (grad_hidden * jax.nn.silu(gate)).astype(bf16)
    grad_gate_w = ring.reduce(normed_two_full, grad_gate)
    grad_up_w = ring.reduce(normed_two_full, grad_upper)

    def grad_normed_rows(span):
        return matmul_nt(grad_gate[span], gate_all) + matmul_nt(grad_upper[span], up_all)

    grad_normed_two = rows_reduce(
        grad_normed_rows(slice(near_rows, None)), grad_normed_rows(slice(0, near_rows))
    )
    grad_middle_norm, grad_gain_two = norm_back(middle, gain_two, grad_normed_two)
    grad_middle = grad_out + grad_middle_norm
    grad_middle_full = rows_gather(grad_middle.astype(bf16))
    heads_rel = jnp.concatenate([heads_near, heads_far], axis=0)
    grad_out_w = ring.reduce(grad_middle_full, heads_rel)
    grad_heads_rel = matmul(grad_middle_full, out_all).astype(bf16)
    grad_heads = jnp.concatenate([block_of(grad_heads_rel, k) for k in range(tp_ways)], axis=0)
    grad_query_parts = []
    grad_keys = jnp.zeros((pack_rows, kv_local, HD), jnp.float32)
    grad_values = jnp.zeros((pack_rows, kv_local, HD), jnp.float32)
    for block_index, first_row in enumerate(starts):
        query_part, span, scores = block_scores(first_row)
        probs = jnp.exp(scores - log_sums[block_index])
        probs_low = probs.astype(jnp.bfloat16)
        grad_part = grad_heads[first_row : first_row + block_rows].reshape(
            block_rows, kv_local, group_size, HD
        )
        grad_probs = jnp.einsum(
            "bngd,snd->ngbs", grad_part, values[span], preferred_element_type=jnp.float32
        )
        inner = jnp.sum(probs * grad_probs, axis=-1, keepdims=True)
        grad_scores = (probs * (grad_probs - inner)).astype(jnp.bfloat16)
        grad_query_parts.append(
            0.125
            * jnp.einsum(
                "ngbs,snd->bngd", grad_scores, keys[span], preferred_element_type=jnp.float32
            )
        )
        grad_keys = grad_keys.at[span].add(
            0.125
            * jnp.einsum(
                "ngbs,bngd->snd", grad_scores, query_part, preferred_element_type=jnp.float32
            )
        )
        grad_values = grad_values.at[span].add(
            jnp.einsum("ngbs,bngd->snd", probs_low, grad_part, preferred_element_type=jnp.float32)
        )
    grad_query = jnp.concatenate(grad_query_parts, axis=0).reshape(pack_rows, heads_local, HD)
    grad_query_low = (
        rotate_back(grad_query, cosine, sine)
        .reshape(pack_rows, heads_local * HD)
        .astype(jnp.bfloat16)
    )
    grad_keys_low = (
        rotate_back(grad_keys, cosine, sine).reshape(pack_rows, kv_local * HD).astype(jnp.bfloat16)
    )
    grad_values_low = grad_values.reshape(pack_rows, kv_local * HD).astype(jnp.bfloat16)
    grad_qkv = jnp.concatenate([grad_query_low, grad_keys_low, grad_values_low], axis=1)
    grad_qkv_w = ring.reduce(normed_full, grad_qkv)
    grad_far = jnp.concatenate([block_of(grad_qkv, 2), block_of(grad_qkv, 3)], axis=0)
    grad_near = jnp.concatenate([block_of(grad_qkv, 0), block_of(grad_qkv, 1)], axis=0)
    grad_normed = rows_reduce(matmul_nt(grad_far, qkv_all), matmul_nt(grad_near, qkv_all))
    grad_input_norm, grad_gain_one = norm_back(inputs32, gain_one, grad_normed)
    grad_inputs = ring.from_ring(grad_middle + grad_input_norm)
    gain_grads = ring.from_ring(jnp.stack([grad_gain_one, grad_gain_two]))
    gain_grads = butterfly(butterfly(gain_grads, "tp"), "fsdp")
    gain_rows = gain_grads.shape[1] // (tp_ways * ring.ways)
    gain_grads = lax.dynamic_slice_in_dim(
        gain_grads, (lax.axis_index("fsdp") * tp_ways + tp_index) * gain_rows, gain_rows, axis=1
    )
    outputs = ring.from_ring(result.astype(bf16))
    return (
        outputs,
        grad_inputs,
        gain_grads[0],
        gain_grads[1],
        grad_qkv_w[:, :q_cols],
        grad_qkv_w[:, q_cols : q_cols + kv_cols],
        grad_qkv_w[:, q_cols + kv_cols :],
        grad_out_w.T,
        grad_gate_w,
        grad_up_w,
        grad_down.T,
    )


def solution(mesh):
    return jax.shard_map(
        per_device,
        mesh=mesh,
        in_specs=(
            P(("fsdp", "tp"), None),
            P(("fsdp", "tp"), None),
            P("fsdp"),
            P("fsdp"),
            P("fsdp", "tp"),
            P("fsdp", "tp"),
            P("fsdp", "tp"),
            P("tp", "fsdp"),
            P("fsdp", "tp"),
            P("fsdp", "tp"),
            P("tp", "fsdp"),
            P("fsdp", None),
            P("fsdp", None),
            P("fsdp"),
        ),
        out_specs=(
            P(("fsdp", "tp"), None),
            P(("fsdp", "tp"), None),
            P(("fsdp", "tp")),
            P(("fsdp", "tp")),
            P("fsdp", "tp"),
            P("fsdp", "tp"),
            P("fsdp", "tp"),
            P("tp", "fsdp"),
            P("fsdp", "tp"),
            P("fsdp", "tp"),
            P("tp", "fsdp"),
        ),
        check_vma=False,
    )
```

```python
import math

import jax
import jax.numpy as jnp
import numpy as np
from jax import lax
from jax.experimental import pallas as pl
from jax.experimental.pallas import tpu as pltpu
from jax.sharding import PartitionSpec as P

HD = 64

epsilon = 1e-05
f32 = jnp.float32
bf16 = jnp.bfloat16


def rope_freqs(head_size):
    base = 1.0 / 500000.0 ** (np.arange(0, head_size, 2) / head_size)
    wavelen = 2.0 * math.pi / base
    smooth = (8192.0 / wavelen - 1.0) / 3.0
    mixed = (1.0 - smooth) * base / 32.0 + smooth * base
    scaled = np.where(wavelen > 8192.0, base / 32.0, np.where(wavelen < 2048.0, base, mixed))
    return jnp.asarray(scaled, dtype=jnp.float32)


def rope_tables(place, head_size):
    angle = place.astype(jnp.float32)[:, None] * rope_freqs(head_size)[None, :]
    cosine = jnp.concatenate([jnp.cos(angle), jnp.cos(angle)], axis=-1)
    sine = jnp.concatenate([jnp.sin(angle), jnp.sin(angle)], axis=-1)
    return (cosine, sine)


def rotate(values, cosine, sine):
    half = values.shape[-1] // 2
    turned = jnp.concatenate([-values[..., half:], values[..., :half]], axis=-1)
    return values * cosine[:, None, :] + turned * sine[:, None, :]


def rotate_back(grads, cosine, sine):
    half = grads.shape[-1] // 2
    turned = grads * sine[:, None, :]
    return grads * cosine[:, None, :] + jnp.concatenate(
        [turned[..., half:], -turned[..., :half]], axis=-1
    )


def rms_norm(values, gain):
    return values * lax.rsqrt(jnp.mean(values * values, axis=-1, keepdims=True) + epsilon) * gain


def norm_back(values, gain, upstream):
    factor = lax.rsqrt(jnp.mean(values * values, axis=-1, keepdims=True) + epsilon)
    normed = values * factor
    scaled = upstream * gain
    grad_values = factor * (scaled - normed * jnp.mean(scaled * normed, axis=-1, keepdims=True))
    return (grad_values, jnp.sum(upstream * normed, axis=0))


def matmul(left, right):
    return jnp.dot(left, right, preferred_element_type=jnp.float32)


def matmul_tn(left, right):
    return lax.dot_general(
        left, right, (((0,), (0,)), ((), ())), preferred_element_type=jnp.float32
    )


def matmul_nt(left, right):
    return lax.dot_general(
        left, right, (((1,), (1,)), ((), ())), preferred_element_type=jnp.float32
    )


def tie(values, *after):
    return lax.optimization_barrier((values, after))[0]


def move_blocks(values, source, width):
    blocks = values.shape[1] // width
    if width % 128 != 0:
        parts = [
            lax.dynamic_slice_in_dim(values, source[j] * width, width, axis=1)
            for j in range(blocks)
        ]
        return jnp.concatenate(parts, axis=1)

    def body(source_ref, values_ref, out_ref):
        for j in range(blocks):
            start = pl.multiple_of(source_ref[j] * width, width)
            out_ref[:, j * width : (j + 1) * width] = values_ref[:, pl.ds(start, width)]

    return pl.pallas_call(
        body,
        out_shape=jax.ShapeDtypeStruct(values.shape, values.dtype),
        in_specs=[
            pl.BlockSpec(memory_space=pltpu.SMEM),
            pl.BlockSpec(memory_space=pltpu.VMEM),
        ],
        out_specs=pl.BlockSpec(memory_space=pltpu.VMEM),
        name="move_blocks",
    )(source, values)


class Ring:
    def __init__(self, axis):
        self.axis = axis
        self.ways = lax.axis_size(axis)
        ways = self.ways
        self.order = list(range(0, ways, 2)) + list(range(1, ways, 2))[::-1]
        places = jnp.asarray([self.order.index(shard) for shard in range(ways)], jnp.int32)
        place = places[lax.axis_index(axis)]
        self.up = [(self.order[i], self.order[(i + 1) % ways]) for i in range(ways)]
        self.down = [(b, a) for a, b in self.up]
        steps = jnp.arange(ways, dtype=jnp.int32)
        order = jnp.asarray(self.order, jnp.int32)
        self.source = jnp.stack(
            [order[(place - steps) % ways] * 2, order[(place + steps) % ways] * 2 + 1], axis=1
        ).reshape(-1)
        self.target = jnp.stack(
            [(place - places) % ways * 2, (places - place) % ways * 2 + 1], axis=1
        ).reshape(-1)

    def to_ring(self, values):
        return move_blocks(values, self.source, values.shape[1] // self.ways // 2)

    def from_ring(self, values):
        return move_blocks(values, self.target, values.shape[1] // self.ways // 2)


class Gathering:
    def __init__(self, ring, shard):
        self.ring = ring
        half = shard.shape[0] // 2
        self.rising, self.falling = [shard[:half]], [shard[half:]]

    def advance(self, *after):
        rising, falling = self.rising[-1], self.falling[-1]
        if after:
            rising, falling = tie((rising, falling), *after)
        self.rising.append(lax.ppermute(rising, self.ring.axis, self.ring.up))
        self.falling.append(lax.ppermute(falling, self.ring.axis, self.ring.down))

    def whole(self):
        while len(self.rising) < self.ring.ways:
            self.advance()
        pairs = zip(self.rising, self.falling)
        return jnp.concatenate([half for pair in pairs for half in pair], axis=0)


def ring_terms(left, block, right, arrived, last):
    rows, columns = right.shape
    tile = min(columns, 1024 if columns % 1024 == 0 else columns)
    half = left.shape[1] // block[1] // 2
    if half % 64 != 0:
        sides = []
        for side in range(2):
            start = (2 * block[0] + side) * half
            term = matmul_tn(left[:, start : start + half], right)
            if arrived:
                term = term + arrived[side].astype(f32)
            sides.append(term if last else term.astype(bf16))
        return [jnp.concatenate(sides, axis=0)] if last else sides

    def body(left_ref, right_ref, *refs):
        turned = refs[-1]

        @pl.when(pl.program_id(0) == 0)
        def _():
            turned[...] = left_ref[...].T

        term = jnp.dot(turned[...], right_ref[...], preferred_element_type=f32)
        for side in range(2):
            part = term[side * half : (side + 1) * half]
            if arrived:
                part = part + refs[side][...].astype(f32)
            if last:
                refs[-2][side * half : (side + 1) * half, :] = part
            else:
                refs[side - 3][...] = part.astype(bf16)

    moving = pl.BlockSpec((half, tile), lambda j: (0, j))
    out_specs = [pl.BlockSpec((2 * half, tile), lambda j: (0, j))] if last else [moving] * 2
    out_shape = (
        [jax.ShapeDtypeStruct((2 * half, columns), f32)]
        if last
        else [jax.ShapeDtypeStruct((half, columns), bf16)] * 2
    )
    return pl.pallas_call(
        body,
        out_shape=out_shape,
        grid=(columns // tile,),
        in_specs=[
            pl.BlockSpec((rows, 2 * half), lambda j: (0, block[0])),
            pl.BlockSpec((rows, tile), lambda j: (0, j)),
        ]
        + [moving] * len(arrived),
        out_specs=out_specs,
        scratch_shapes=[pltpu.VMEM((2 * half, rows), bf16)],
        cost_estimate=pl.CostEstimate(
            flops=4 * half * rows * columns,
            bytes_accessed=2 * rows * (columns + 2 * half) + 8 * half * columns,
            transcendentals=0,
        ),
        name="ring_terms",
    )(left, right, *arrived)


class Reduction:
    def __init__(self, ring, left, right):
        self.ring, self.left, self.right = ring, left, right
        self.step, self.totals = 0, []

    def advance(self, *after):
        ways = self.ring.ways
        if self.step >= ways:
            return ()
        left = tie(self.left, *after) if after else self.left
        arrived = [
            lax.ppermute(total, self.ring.axis, hop)
            for total, hop in zip(self.totals, (self.ring.up, self.ring.down))
        ]
        block = ((1 + self.step) % ways, ways)
        self.totals = ring_terms(left, block, self.right, arrived, self.step == ways - 1)
        self.step += 1
        return tuple(self.totals)

    def whole(self):
        while self.step < self.ring.ways:
            self.advance()
        return self.totals[0]


def advance(value, *reductions):
    tokens = []
    for reduction in reductions:
        tokens += reduction.advance(value)
    return tie(value, *tokens) if tokens else value


def swap(values, axis, bit):
    return lax.ppermute(values, axis, [(i, i ^ bit) for i in range(lax.axis_size(axis))])


def butterfly(values, axis):
    bit = 1
    while bit < lax.axis_size(axis):
        values = values + swap(values, axis, bit)
        bit *= 2
    return values


def rows_gather(rows):
    across = swap(rows, "tp", 2)
    beside = swap(rows, "tp", 1)
    return jnp.concatenate([rows, beside, across, swap(across, "tp", 1)], axis=0)


def rows_reduce(far, near):
    rows = far.shape[0] // 2
    across = far[:rows] + swap(far[rows:].astype(bf16), "tp", 1).astype(f32)
    across = swap(across.astype(bf16), "tp", 2).astype(f32)
    return near[:rows] + swap(near[rows:].astype(bf16), "tp", 1).astype(f32) + across


def per_device(
    inputs,
    teacher,
    gain_attn,
    gain_mlp,
    w_query,
    w_key,
    w_value,
    w_out,
    w_gate,
    w_up,
    w_down,
    position,
    documents,
    lengths,
):
    row_count = inputs.shape[0]
    tp_ways = lax.axis_size("tp")
    pack_rows = row_count * tp_ways
    total_rows = pack_rows * lax.axis_size("fsdp")
    tp_index = lax.axis_index("tp")
    ring = Ring("fsdp")
    place = position[0]
    label = documents[0]

    def own_rows(values):
        return lax.dynamic_slice_in_dim(values, tp_index * row_count, row_count)

    def block_of(values, block):
        return lax.dynamic_slice_in_dim(
            values, (tp_index ^ block) * row_count, row_count
        )

    count = butterfly(jnp.clip(lengths, 0, pack_rows).astype(f32), "fsdp")[0]
    given = jnp.arange(pack_rows, dtype=jnp.int32)
    valid = (own_rows(given) < lengths[0]).astype(f32)
    cosine, sine = rope_tables(given, HD)

    q_cols, kv_cols, out_cols = w_query.shape[1], w_key.shape[1], w_out.shape[0]
    gains = jnp.stack([gain_attn, gain_mlp], axis=1)
    gains = jnp.pad(gains, ((0, 0), (0, 126)))
    held = rows_gather(ring.to_ring(inputs))
    attn_ring = Gathering(
        ring, jnp.concatenate([w_query, w_key, w_value, w_out.T, gains], axis=1)
    )
    attn_all = attn_ring.whole()
    qkv_cols = q_cols + 2 * kv_cols
    qkv_all = attn_all[:, :qkv_cols]
    out_all = attn_all[:, qkv_cols : qkv_cols + out_cols]
    gain_one = attn_all[:, qkv_cols + out_cols].astype(f32)
    gain_two = attn_all[:, qkv_cols + out_cols + 1].astype(f32)
    gate_ring, up_ring = Gathering(ring, w_gate), Gathering(ring, w_up)
    down_ring = Gathering(ring, w_down.T)
    near_last = (attn_ring.rising[-2], attn_ring.falling[-2])
    gate_ring.advance(*near_last)
    up_ring.advance(*near_last)

    def forward_step(value):
        if len(up_ring.rising) < ring.ways:
            gate_ring.advance(value)
            up_ring.advance(value)
        elif len(down_ring.rising) < ring.ways:
            down_ring.advance(value)

    place_blocks = jnp.concatenate([block_of(place, k) for k in range(tp_ways)])
    pick = (given[:, None] == place_blocks[None, :]).astype(bf16)
    inputs_full = matmul(pick, held)
    inputs32 = own_rows(inputs_full)
    normed_full = rms_norm(inputs_full, gain_one).astype(bf16)

    heads_local = q_cols // HD
    kv_local = kv_cols // HD
    group_size = heads_local // kv_local
    qkv = matmul(normed_full, qkv_all)
    forward_step(qkv)
    teacher_own = matmul(own_rows(pick), rows_gather(tie(ring.to_ring(teacher), qkv)))
    query = rotate(qkv[:, :q_cols].reshape(pack_rows, heads_local, HD), cosine, sine).astype(bf16)
    keys = rotate(
        qkv[:, q_cols : q_cols + kv_cols].reshape(pack_rows, kv_local, HD), cosine, sine
    ).astype(bf16)
    values = qkv[:, q_cols + kv_cols :].astype(bf16).reshape(pack_rows, kv_local, HD)
    block_rows = min(256, pack_rows)
    starts = list(range(0, pack_rows, block_rows))
    reach = pack_rows // 2

    def block_scores(first_row):
        first_key = max(0, first_row - reach)
        span = slice(first_key, first_row + block_rows)
        rows = slice(first_row, first_row + block_rows)
        query_part = query[rows].reshape(block_rows, kv_local, group_size, HD)
        scores = 0.125 * jnp.einsum(
            "bngd,snd->ngbs", query_part, keys[span], preferred_element_type=jnp.float32
        )
        allowed = (label[rows][:, None] == label[span][None, :]) & (
            given[span][None, :] <= given[rows][:, None]
        )
        return (query_part, span, jnp.where(allowed[None, None], scores, -1e30))

    head_parts = []
    log_sums = []
    for first_row in starts:
        query_part, span, scores = block_scores(first_row)
        row_max = jnp.max(scores, axis=-1, keepdims=True)
        weights = jnp.exp(scores - row_max)
        row_total = jnp.sum(weights, axis=-1, keepdims=True)
        probs = (weights / row_total).astype(jnp.bfloat16)
        mixed = jnp.einsum("ngbs,snd->bngd", probs, values[span], preferred_element_type=jnp.float32)
        head_parts.append(mixed.astype(jnp.bfloat16).reshape(block_rows, heads_local * HD))
        log_sums.append(row_max + jnp.log(row_total))
        if len(head_parts) % 2 == 0:
            forward_step(head_parts[-1])
    heads = jnp.concatenate(head_parts, axis=0)

    heads_far = jnp.concatenate([block_of(heads, 2), block_of(heads, 3)], axis=0)
    heads_near = jnp.concatenate([block_of(heads, 0), block_of(heads, 1)], axis=0)
    middle = inputs32 + rows_reduce(matmul_nt(heads_far, out_all), matmul_nt(heads_near, out_all))
    normed_two = rms_norm(middle, gain_two).astype(bf16)
    forward_step(normed_two)
    normed_two_full = rows_gather(normed_two)
    forward_step(normed_two_full)
    while len(up_ring.rising) < ring.ways:
        forward_step(normed_two_full)
    down_ring.advance(gate_ring.rising[-2], up_ring.rising[-2])
    gate_all, up_all = gate_ring.whole(), up_ring.whole()
    gate = matmul(normed_two_full, gate_all)
    forward_step(gate)
    upper = matmul(normed_two_full, up_all)
    hidden = (jax.nn.silu(gate) * upper).astype(bf16)
    forward_step(hidden)
    down_all = down_ring.whole()
    near_rows = 2 * row_count
    result = middle + rows_reduce(
        matmul_nt(hidden[near_rows:], down_all), matmul_nt(hidden[:near_rows], down_all)
    )
    grad_out = total_rows / count * valid[:, None] * (result - teacher_own)
    grad_out_full = rows_gather(grad_out.astype(bf16))
    down_sum = Reduction(ring, grad_out_full, hidden)
    grad_out_full = advance(grad_out_full, down_sum)
    grad_hidden = matmul(grad_out_full, down_all)
    sigma = jax.nn.sigmoid(gate)
    grad_gate = (grad_hidden * upper * sigma * (1.0 + gate * (1.0 - sigma))).astype(bf16)
    grad_upper = (grad_hidden * jax.nn.silu(gate)).astype(bf16)
    pair_sum = Reduction(
        ring, normed_two_full, jnp.concatenate([grad_gate, grad_upper], axis=1)
    )
    grad_gate, grad_upper = advance((grad_gate, grad_upper), down_sum, pair_sum)

    def grad_normed_rows(span):
        return matmul_nt(grad_gate[span], gate_all) + matmul_nt(grad_upper[span], up_all)

    far = advance(grad_normed_rows(slice(near_rows, None)), down_sum)
    near = advance(grad_normed_rows(slice(0, near_rows)), pair_sum, down_sum)
    grad_normed_two = rows_reduce(far, near)
    grad_middle_norm, grad_gain_two = norm_back(middle, gain_two, grad_normed_two)
    grad_middle = grad_out + grad_middle_norm
    grad_middle_low = advance(grad_middle.astype(bf16), down_sum, pair_sum)
    grad_middle_full = advance(rows_gather(grad_middle_low), down_sum, pair_sum)
    heads_rel = jnp.concatenate([heads_near, heads_far], axis=0)
    out_sum = Reduction(ring, grad_middle_full, heads_rel)
    grad_heads_rel = matmul(grad_middle_full, out_all).astype(bf16)
    grad_heads_rel = advance(grad_heads_rel, out_sum)
    grad_heads = jnp.concatenate([block_of(grad_heads_rel, k) for k in range(tp_ways)], axis=0)
    grad_query_parts = []
    grad_keys = jnp.zeros((pack_rows, kv_local, HD), jnp.float32)
    grad_values = jnp.zeros((pack_rows, kv_local, HD), jnp.float32)
    for block_index, first_row in enumerate(starts):
        query_part, span, scores = block_scores(first_row)
        probs = jnp.exp(scores - log_sums[block_index])
        probs_low = probs.astype(jnp.bfloat16)
        grad_part = grad_heads[first_row : first_row + block_rows].reshape(
            block_rows, kv_local, group_size, HD
        )
        grad_probs = jnp.einsum(
            "bngd,snd->ngbs", grad_part, values[span], preferred_element_type=jnp.float32
        )
        inner = jnp.sum(probs * grad_probs, axis=-1, keepdims=True)
        grad_scores = (probs * (grad_probs - inner)).astype(jnp.bfloat16)
        grad_query_parts.append(
            0.125
            * jnp.einsum(
                "ngbs,snd->bngd", grad_scores, keys[span], preferred_element_type=jnp.float32
            )
        )
        rings = [(out_sum,), (down_sum, pair_sum), (out_sum,), (pair_sum, down_sum, out_sum)]
        grad_scores = advance(grad_scores, *rings[block_index % 4])
        grad_keys = grad_keys.at[span].add(
            0.125
            * jnp.einsum(
                "ngbs,bngd->snd", grad_scores, query_part, preferred_element_type=jnp.float32
            )
        )
        grad_values = grad_values.at[span].add(
            jnp.einsum("ngbs,bngd->snd", probs_low, grad_part, preferred_element_type=jnp.float32)
        )
    grad_query = jnp.concatenate(grad_query_parts, axis=0).reshape(pack_rows, heads_local, HD)
    grad_query_low = (
        rotate_back(grad_query, cosine, sine)
        .reshape(pack_rows, heads_local * HD)
        .astype(jnp.bfloat16)
    )
    grad_keys_low = (
        rotate_back(grad_keys, cosine, sine).reshape(pack_rows, kv_local * HD).astype(jnp.bfloat16)
    )
    grad_values_low = grad_values.reshape(pack_rows, kv_local * HD).astype(jnp.bfloat16)
    grad_qkv = jnp.concatenate([grad_query_low, grad_keys_low, grad_values_low], axis=1)
    qkv_sum = Reduction(ring, normed_full, grad_qkv)
    grad_qkv = advance(grad_qkv, qkv_sum, out_sum)
    grad_far = jnp.concatenate([block_of(grad_qkv, 2), block_of(grad_qkv, 3)], axis=0)
    grad_near = jnp.concatenate([block_of(grad_qkv, 0), block_of(grad_qkv, 1)], axis=0)
    near = advance(matmul_nt(grad_near, qkv_all), pair_sum, qkv_sum, out_sum)
    near = advance(near, qkv_sum, out_sum)
    grad_normed = rows_reduce(matmul_nt(grad_far, qkv_all), near)
    grad_input_norm, grad_gain_one = norm_back(inputs32, gain_one, grad_normed)
    grad_inputs = ring.from_ring(grad_middle + grad_input_norm)
    gain_grads = ring.from_ring(jnp.stack([grad_gain_one, grad_gain_two]))
    gain_grads = butterfly(butterfly(gain_grads, "tp"), "fsdp")
    gain_rows = gain_grads.shape[1] // (tp_ways * ring.ways)
    gain_grads = lax.dynamic_slice_in_dim(
        gain_grads, (lax.axis_index("fsdp") * tp_ways + tp_index) * gain_rows, gain_rows, axis=1
    )
    outputs = ring.from_ring(result.astype(bf16))
    grad_down, grad_pair = down_sum.whole(), pair_sum.whole()
    grad_out_w, grad_qkv_w = out_sum.whole(), qkv_sum.whole()
    hidden_cols = w_gate.shape[1]
    return (
        outputs,
        grad_inputs,
        gain_grads[0],
        gain_grads[1],
        grad_qkv_w[:, :q_cols],
        grad_qkv_w[:, q_cols : q_cols + kv_cols],
        grad_qkv_w[:, q_cols + kv_cols :],
        grad_out_w.T,
        grad_pair[:, :hidden_cols],
        grad_pair[:, hidden_cols:],
        grad_down.T,
    )


def solution(mesh):
    return jax.shard_map(
        per_device,
        mesh=mesh,
        in_specs=(
            P(("fsdp", "tp"), None),
            P(("fsdp", "tp"), None),
            P("fsdp"),
            P("fsdp"),
            P("fsdp", "tp"),
            P("fsdp", "tp"),
            P("fsdp", "tp"),
            P("tp", "fsdp"),
            P("fsdp", "tp"),
            P("fsdp", "tp"),
            P("tp", "fsdp"),
            P("fsdp", None),
            P("fsdp", None),
            P("fsdp"),
        ),
        out_specs=(
            P(("fsdp", "tp"), None),
            P(("fsdp", "tp"), None),
            P(("fsdp", "tp")),
            P(("fsdp", "tp")),
            P("fsdp", "tp"),
            P("fsdp", "tp"),
            P("fsdp", "tp"),
            P("tp", "fsdp"),
            P("fsdp", "tp"),
            P("fsdp", "tp"),
            P("tp", "fsdp"),
        ),
        check_vma=False,
    )
```
